32 devices in a mesh: replica: 2 (over y), ctx: 4 (over z), head: 2 (over x), sub: 2 (over core).
Axes of the slice: x: 2, y: 2, z: 4, core: 2. Of those that a mesh axis runs over, the one named last changes fastest.
Arguments:
- queries: bfloat16 [8192, 2048], P(('replica', 'ctx', 'sub'), 'head'), parts along dimension 0, may hold values from -64 to 64
- keys: bfloat16 [8192, 1024], P(('replica', 'ctx', 'sub'), 'head'), parts along dimension 0, may hold values from -16 to 16
- values: bfloat16 [8192, 1024], P(('replica', 'ctx', 'sub'), 'head'), parts along dimension 0, may hold values from -6 to 6
- segment: int32 [8192], P(('replica', 'ctx', 'sub')), parts along dimension 0, may hold values from 0 to 1, as said below
- cotangent: bfloat16 [8192, 2560], P(('replica', 'ctx', 'sub')), parts along dimension 0, may hold values from -96 to 96
- out_weight: bfloat16 [2560, 2048], P(None, 'head'), may hold values from -0.125 to 0.125
Outputs:
- grad_queries: bfloat16 [8192, 2048], P(('replica', 'ctx', 'sub'), 'head'), parts along dimension 0
- grad_keys: bfloat16 [8192, 1024], P(('replica', 'ctx', 'sub'), 'head'), parts along dimension 0
- grad_values: bfloat16 [8192, 1024], P(('replica', 'ctx', 'sub'), 'head'), parts along dimension 0
- grad_out_weight: float32 [5120, 2048], P(('replica', 'ctx', 'sub'), 'head'), parts along dimension 0
The draws below stay inside these ranges and needn't reach their ends.
There are 2 independent parts, one for each index of `replica`. The reference program is written for one: setup_inputs(seed, part) draws one part's arguments, and reference() takes and returns one part's arrays. A program takes and returns all parts, laid end to end along the dimension named above; an argument that names none is the same for every part. Nothing has to cross between parts.
Inputs may be any that keep to these rules, and one draw needn't show every extreme that they name: segment numbers start at 0, never fall along the sequence and rise by one at the first token of each document; the last document's number is the max.
All inputs are finite; a program needn't handle non-finite values.
Results may differ from the reference program's by a relative error of at most 0.018.
Values may be sent and summed in bfloat16 or wider, within the bound.
A program may use at most 128 MiB of HBM per device.

```python
import jax
import jax.numpy as jnp
from jax import lax

D = 2560
HEADS = 8
KV_HEADS = 4
DH = 256
WINDOW = 1024
TOK_DEV = 512
DOC = 2048
TOKENS = 4096


def segment_ids(key):
    doc_starts = max(TOKENS // DOC - 1, 1)
    chosen = jax.random.permutation(jax.random.fold_in(key, 11), TOKENS - 1)[:doc_starts] + 1
    opening = jnp.zeros((TOKENS,), jnp.int32).at[chosen].set(1)
    return jnp.cumsum(opening).astype(jnp.int32)


def drawn_keys(key):
    return jnp.clip(jax.random.normal(jax.random.fold_in(key, 21), (TOKENS, KV_HEADS * DH), jnp.float32), -4.0, 4.0)


def draw_segment(key, part):
    return segment_ids(key)


def draw_keys(key, part):
    base_keys = drawn_keys(key)
    return base_keys.astype(jnp.bfloat16)


def draw_queries(key, part):
    base_queries = jnp.clip(jax.random.normal(jax.random.fold_in(key, 22), (TOKENS, HEADS * DH), jnp.float32), -4.0, 4.0)
    return base_queries.astype(jnp.bfloat16)


def strengthened(array, key, source, target, blocks, factor):
    owner, partner = [(jnp.arange(array.shape[dim]) // (array.shape[dim] // blocks)).reshape([-1 if axis == dim else 1 for axis in range(array.ndim)]) for dim in (source, target)]
    chosen = jax.random.permutation(key, blocks)[partner]
    strong = (owner == chosen) | (owner == (partner + blocks // 2) % blocks)
    return jnp.where(strong, factor * array, array)


def level_of(own_key, extent, cuts, smallest, largest):
    loudness, own = 1.0, jax.random.fold_in(own_key, 6)
    for axis_at, shards_of in cuts:
        steps = jnp.exp(jax.random.uniform(jax.random.fold_in(own, axis_at), (shards_of,), jnp.float32, smallest / len(cuts), largest / len(cuts)))
        loudness = loudness * jnp.repeat(steps, extent[axis_at] // shards_of).reshape([-1 if axis == axis_at else 1 for axis in range(len(extent))])
    return loudness


def noise(rng, dims, scale, reach, cuts=(), held_as=jnp.bfloat16):
    factor_of = level_of(rng, dims, cuts, -0.22, 0.18) if cuts else 1.0
    array = jax.random.normal(rng, dims, jnp.float32) * scale * factor_of
    return jnp.minimum(jnp.maximum(array, -reach), reach).astype(held_as)


def heavy_noise(rng, extent, scale, limit, split, heavy, kind=jnp.bfloat16):
    values = scale * jax.random.normal(rng, extent, jnp.float32)
    if split:
        values = values * level_of(rng, extent, split, -0.22, 0.18)
    return jnp.clip(strengthened(values, jax.random.fold_in(rng, 3), *heavy), -limit, limit).astype(kind)


def setup_inputs(seed: int = 0, part: int = 0) -> dict:
    arg_keys = jax.random.split(jax.random.key(seed), 7)
    part_keys = jax.random.split(jax.random.fold_in(arg_keys[6], part), 7)
    return {
        "queries": draw_queries(jax.random.fold_in(jax.random.fold_in(arg_keys[6], part), 71), part),
        "keys": draw_keys(jax.random.fold_in(jax.random.fold_in(arg_keys[6], part), 71), part),
        "values": noise(part_keys[2], (TOKENS, KV_HEADS * DH), 1.0, 6.0, ((0, 8), (1, 2))),
        "segment": draw_segment(jax.random.fold_in(jax.random.fold_in(arg_keys[6], part), 71), part),
        "cotangent": heavy_noise(part_keys[4], (TOKENS, D), 16.0, 96.0, ((0, 8),), (0, 1, 8, 2.0)),
        "out_weight": noise(arg_keys[5], (D, HEADS * DH), (HEADS * DH) ** -0.5, 0.125, ((1, 2),)),
    }


def reference(queries, keys, values, segment, cotangent, out_weight):
    groups = HEADS // KV_HEADS
    score_scale = DH ** -0.5
    span_keys = WINDOW + TOK_DEV
    block_count = TOKENS // TOK_DEV
    attention_grad_all = jnp.dot(cotangent, out_weight, preferred_element_type=jnp.float32).astype(jnp.bfloat16)
    key_pad = jnp.concatenate([jnp.zeros((WINDOW, KV_HEADS * DH), keys.dtype), keys], 0)
    value_pad = jnp.concatenate([jnp.zeros((WINDOW, KV_HEADS * DH), values.dtype), values], 0)
    segment_pad = jnp.concatenate([jnp.full((WINDOW,), -1, jnp.int32), segment.astype(jnp.int32)], 0)

    def one_block(carry, block):
        key_acc, value_acc = carry
        block_start = (block * TOK_DEV).astype(jnp.int32)
        query_block = lax.dynamic_slice_in_dim(queries, block_start, TOK_DEV, 0)
        grad_block = lax.dynamic_slice_in_dim(attention_grad_all, block_start, TOK_DEV, 0)
        query_segment = lax.dynamic_slice_in_dim(segment.astype(jnp.int32), block_start, TOK_DEV, 0)
        key_block = lax.dynamic_slice_in_dim(key_pad, block_start, span_keys, 0)
        value_block = lax.dynamic_slice_in_dim(value_pad, block_start, span_keys, 0)
        key_segment = lax.dynamic_slice_in_dim(segment_pad, block_start, span_keys, 0)
        query_pos = block_start + jnp.arange(TOK_DEV, dtype=jnp.int32)
        key_pos = block_start - WINDOW + jnp.arange(span_keys, dtype=jnp.int32)
        allowed = (key_pos[None, :] >= 0) & (key_pos[None, :] <= query_pos[:, None])
        allowed = allowed & (query_pos[:, None] - key_pos[None, :] < WINDOW)
        allowed = allowed & (query_segment[:, None] == key_segment[None, :])
        query_heads = query_block.astype(jnp.float32).reshape(TOK_DEV, KV_HEADS, groups, DH)
        key_heads = key_block.astype(jnp.float32).reshape(span_keys, KV_HEADS, DH)
        value_heads = value_block.astype(jnp.float32).reshape(span_keys, KV_HEADS, DH)
        grad_heads = grad_block.astype(jnp.float32).reshape(TOK_DEV, KV_HEADS, groups, DH)
        scores = jnp.einsum("qkgd,skd->kgqs", query_heads, key_heads) * score_scale
        scores = jnp.where(allowed[None, None], scores, -jnp.inf)
        row_max = jnp.max(scores, axis=-1, keepdims=True)
        log_total = row_max + jnp.log(jnp.sum(jnp.exp(scores - row_max), axis=-1, keepdims=True))
        softmax = jnp.exp(scores - log_total)
        rounded_softmax = softmax.astype(jnp.bfloat16)
        attention = jnp.einsum("kgqs,skd->qkgd", rounded_softmax.astype(jnp.float32), value_heads).astype(jnp.bfloat16)
        row_dot = jnp.transpose(jnp.sum(attention.astype(jnp.float32) * grad_heads, axis=-1), (1, 2, 0))
        softmax_grad = jnp.einsum("qkgd,skd->kgqs", grad_heads, value_heads)
        score_grad = (softmax * (softmax_grad - row_dot[..., None])).astype(jnp.bfloat16)
        query_grad = (jnp.einsum("kgqs,skd->qkgd", score_grad.astype(jnp.float32), key_heads) * score_scale).astype(jnp.bfloat16)
        key_terms = jnp.einsum("kgqs,qkgd->skd", score_grad.astype(jnp.float32), query_heads) * score_scale
        value_terms = jnp.einsum("kgqs,qkgd->skd", rounded_softmax.astype(jnp.float32), grad_heads)
        key_terms = key_terms.reshape(span_keys, KV_HEADS * DH)
        value_terms = value_terms.reshape(span_keys, KV_HEADS * DH)
        key_acc = lax.dynamic_update_slice_in_dim(key_acc, lax.dynamic_slice_in_dim(key_acc, block_start, span_keys, 0) + key_terms, block_start, 0)
        value_acc = lax.dynamic_update_slice_in_dim(value_acc, lax.dynamic_slice_in_dim(value_acc, block_start, span_keys, 0) + value_terms, block_start, 0)
        return (key_acc, value_acc), (query_grad.reshape(TOK_DEV, HEADS * DH), attention.reshape(TOK_DEV, HEADS * DH))

    start_acc = jnp.zeros((TOKENS + WINDOW, KV_HEADS * DH), jnp.float32)
    (key_acc, value_acc), (query_grads, attentions) = lax.scan(one_block, (start_acc, start_acc), jnp.arange(block_count, dtype=jnp.int32))
    grad_queries = query_grads.reshape(TOKENS, HEADS * DH)
    attention_all = attentions.reshape(TOKENS, HEADS * DH)
    grad_keys = key_acc[WINDOW:].astype(jnp.bfloat16)
    grad_values = value_acc[WINDOW:].astype(jnp.bfloat16)
    grad_out_weight = jnp.dot(cotangent.T, attention_all, preferred_element_type=jnp.float32) * (TOKENS ** -0.5)
    return (grad_queries, grad_keys, grad_values, grad_out_weight)
```

```python
import functools

import jax
import jax.numpy as jnp
from jax import lax
from jax.experimental import pallas as pl
from jax.experimental.pallas import tpu as pltpu
from jax.sharding import PartitionSpec as P

DH = 256
WINDOW = 1024
QB = 256
SPAN = WINDOW + QB
MASKED = -1e30
MESH = pl.DeviceIdType.MESH
F32 = jnp.float32
BF16 = jnp.bfloat16


def dot_nt(a, b):
    return lax.dot_general(a, b, (((1,), (1,)), ((), ())), preferred_element_type=F32)


def dot_tn(a, b):
    return lax.dot_general(a, b, (((0,), (0,)), ((), ())), preferred_element_type=F32)


def dot_nn(a, b):
    return lax.dot_general(a, b, (((1,), (0,)), ((), ())), preferred_element_type=F32)


def layer_kernel(
    nz, ng, groups, norm,
    q_hbm, k_hbm, v_hbm, seg_hbm, cot_hbm, w_hbm,
    dq_ref, dk_ref, dv_ref, gow_ref,
    q_s, w_s, cot_s, cot_t, da_s, at_s, kall, vall, seg_s, bias_s, prob_s, dk_acc, dv_acc,
    mid_send, mid_recv, back_send, back_recv,
    own_part, pair_send, pair_recv, far_send, far_recv, own_sum,
    in_sem, halo_ss, halo_rs, fwd_ss, fwd_rs, mid_ss, mid_rs, back_ss, back_rs,
    pair_ss, pair_rs, far_ss, far_rs,
):
    heads = ng * groups
    rows = q_hbm.shape[0]
    width = cot_hbm.shape[1]
    part = width // (2 * nz)
    scale = DH ** -0.5
    z = lax.axis_index("ctx")
    s = lax.axis_index("sub")
    peer = 1 - s
    above = lax.rem(z + 1, nz)
    below = lax.rem(z + nz - 1, nz)
    has_above = z < nz - 1
    has_below = z > 0

    def cols(h):
        return pl.ds(h * DH, DH)

    loads = []

    def load(src, dst):
        copy = pltpu.make_async_copy(src, dst, in_sem.at[len(loads)])
        copy.start()
        loads.append(copy)
        return copy

    load_seg = load(seg_hbm, seg_s.at[2])
    load_cot = load(cot_hbm, cot_s)
    load_w = [load(w_hbm.at[:, cols(h)], w_s.at[h]) for h in range(heads)]
    load_kv = [
        (
            load(k_hbm.at[:, cols(g)], kall.at[g, pl.ds(2 * rows, rows)]),
            load(v_hbm.at[:, cols(g)], vall.at[g, pl.ds(2 * rows, rows)]),
        )
        for g in range(ng)
    ]
    load_q = [load(q_hbm.at[:, cols(h)], q_s.at[h]) for h in range(heads)]

    barrier = pltpu.get_barrier_semaphore()
    for step in range(1, nz):
        pl.semaphore_signal(barrier, inc=1, device_id={"ctx": lax.rem(z + step, nz)}, device_id_type=MESH)
    pl.semaphore_signal(barrier, inc=1, device_id={"sub": peer}, device_id_type=MESH)
    pl.semaphore_wait(barrier, nz)

    def halo(i, src, dst):
        return pltpu.make_async_remote_copy(
            src_ref=src, dst_ref=dst, send_sem=halo_ss.at[i], recv_sem=halo_rs.at[i],
            device_id={"ctx": above}, device_id_type=MESH,
        )

    def forward(i, src, dst):
        return pltpu.make_async_remote_copy(
            src_ref=src, dst_ref=dst, send_sem=fwd_ss.at[i], recv_sem=fwd_rs.at[i],
            device_id={"sub": peer}, device_id_type=MESH,
        )

    first, middle = pl.ds(0, rows), pl.ds(rows, rows)
    seg_i = 2 * ng
    halos = [halo(seg_i, seg_hbm, seg_s.at[0])]
    from_own = [forward(seg_i, seg_hbm, seg_s.at[1])]
    from_halo = [forward(seg_i, seg_s.at[0], seg_s.at[1])]
    for g in range(ng):
        for j, (hbm, both) in enumerate(((k_hbm, kall), (v_hbm, vall))):
            i = 2 * g + j
            halos.append(halo(i, hbm.at[:, cols(g)], both.at[g, first]))
            from_own.append(forward(i, hbm.at[:, cols(g)], both.at[g, middle]))
            from_halo.append(forward(i, both.at[g, first], both.at[g, middle]))

    @pl.when(has_above)
    def _():
        for copy in halos:
            copy.start()

    @pl.when(s == 0)
    def _():
        for copy in from_own:
            copy.start()

    @pl.when(jnp.logical_not(has_below))
    def _():
        seg_s[0] = jnp.full((1, rows), -1, jnp.int32)
        for g in range(ng):
            kall[g, first] = jnp.zeros((rows, DH), BF16)
            vall[g, first] = jnp.zeros((rows, DH), BF16)

    @pl.when(jnp.logical_not(has_below) & (s == 0))
    def _():
        seg_s[1] = jnp.full((1, rows), -1, jnp.int32)
        for g in range(ng):
            kall[g, middle] = jnp.zeros((rows, DH), BF16)
            vall[g, middle] = jnp.zeros((rows, DH), BF16)

    def arrive(indices):
        @pl.when(has_below)
        def _():
            for i in indices:
                halos[i].wait_recv()

        @pl.when(has_below & (s == 1))
        def _():
            for i in indices:
                from_halo[i].start()

        @pl.when(has_below | (s == 1))
        def _():
            for i in indices:
                from_halo[i].wait_recv()

    load_cot.wait()
    for h in range(heads):
        load_w[h].wait()

    def attention_grad(h, carry):
        da_s[h] = dot_nn(cot_s[...], w_s[h]).astype(BF16)
        return carry

    lax.fori_loop(0, heads, attention_grad, 0)

    for j in range(width // DH):
        cot_t[pl.ds(j * DH, DH)] = cot_s[:, cols(j)].T

    load_seg.wait()
    arrive([0])
    for b in range(rows // QB):
        own = seg_s[2]
        keys_row = jnp.concatenate([seg_s[0], seg_s[1], own], axis=1)[:, b * QB : b * QB + SPAN]
        column = jnp.broadcast_to(own[:, b * QB : (b + 1) * QB].astype(F32), (128, QB)).T[:, :1]
        at_query = lax.broadcasted_iota(jnp.int32, (QB, SPAN), 0)
        at_key = lax.broadcasted_iota(jnp.int32, (QB, SPAN), 1)
        allowed = (at_key > at_query) & (at_key <= at_query + WINDOW)
        allowed = allowed & (column == keys_row.astype(F32))
        bias_s[b] = jnp.where(allowed, 0.0, MASKED)

    def mid_copy(g, j):
        return pltpu.make_async_remote_copy(
            src_ref=mid_send.at[g, j], dst_ref=mid_recv.at[g, j],
            send_sem=mid_ss.at[g, j], recv_sem=mid_rs.at[g, j],
            device_id={"sub": peer}, device_id_type=MESH,
        )

    def back_copy(g, j):
        return pltpu.make_async_remote_copy(
            src_ref=back_send.at[g, j], dst_ref=back_recv.at[g, j],
            send_sem=back_ss.at[g, j], recv_sem=back_rs.at[g, j],
            device_id={"ctx": below}, device_id_type=MESH,
        )

    def pair_copy(h):
        return pltpu.make_async_remote_copy(
            src_ref=pair_send.at[h], dst_ref=pair_recv.at[h],
            send_sem=pair_ss.at[h], recv_sem=pair_rs.at[h],
            device_id={"sub": peer}, device_id_type=MESH,
        )

    def far_send_copy(h, d):
        return pltpu.make_async_remote_copy(
            src_ref=far_send.at[h, d], dst_ref=far_recv.at[h, z],
            send_sem=far_ss.at[h, d], recv_sem=far_rs.at[h, z],
            device_id={"ctx": d}, device_id_type=MESH,
        )

    def far_recv_copy(h, d):
        return pltpu.make_async_remote_copy(
            src_ref=far_send.at[h, d], dst_ref=far_recv.at[h, d],
            send_sem=far_ss.at[h, d], recv_sem=far_rs.at[h, d],
            device_id={"ctx": d}, device_id_type=MESH,
        )

    def part_rows(d, side):
        return pl.ds(pl.multiple_of((d * 2 + side) * part, 16), part)

    def send_back(g):
        for j, acc in enumerate((dk_acc, dv_acc)):
            mid_copy(g, j).wait_recv()
            other = mid_recv[g, j].astype(F32)
            back_send[g, j] = (acc[g, first] + jnp.where(s == 1, other, 0.0)).astype(BF16)

            @pl.when(has_below)
            def _():
                back_copy(g, j).start()

            last = pl.ds(2 * rows, rows)
            acc[g, last] = acc[g, last] + jnp.where(s == 0, other, 0.0)

    for g in range(ng):
        load_kv[g][0].wait()
        load_kv[g][1].wait()
        arrive([1 + 2 * g, 2 + 2 * g])
        dk_acc[g] = jnp.zeros((3 * rows, DH), F32)
        dv_acc[g] = jnp.zeros((3 * rows, DH), F32)
        for h in range(g * groups, (g + 1) * groups):
            load_q[h].wait()

            def attend(b, carry):
                mine = pl.ds(pl.multiple_of(b * QB, QB), QB)
                reach = pl.ds(pl.multiple_of(b * QB, QB), SPAN)
                scores = dot_nt(q_s[h, mine], kall[g, reach]) * scale + bias_s[b]
                top = jnp.max(scores, axis=1, keepdims=True)
                raised = jnp.exp(scores - top)
                probs = raised * (1.0 / jnp.sum(raised, axis=1, keepdims=True))
                prob_s[b] = probs
                at_s[mine] = dot_nn(probs.astype(BF16), vall[g, reach]).astype(BF16)
                return carry

            lax.fori_loop(0, rows // QB, attend, 0)

            def weight_part(d, carry):
                pair_send[h, d] = dot_nn(cot_t[part_rows(d, peer)], at_s[...]).astype(BF16)
                return carry

            lax.fori_loop(0, nz, weight_part, 0)
            pair_copy(h).start()

            def weight_own(d, carry):
                own_part[d] = dot_nn(cot_t[part_rows(d, s)], at_s[...])
                return carry

            lax.fori_loop(0, nz, weight_own, 0)

            def attend_back(b, carry):
                mine = pl.ds(pl.multiple_of(b * QB, QB), QB)
                reach = pl.ds(pl.multiple_of(b * QB, QB), SPAN)
                grad = da_s[h, mine]
                probs = prob_s[b]
                delta = jnp.sum(at_s[mine].astype(F32) * grad.astype(F32), axis=1, keepdims=True)
                dscores = (probs * (dot_nt(grad, vall[g, reach]) - delta)).astype(BF16)
                dq_ref[mine, cols(h)] = (dot_nn(dscores, kall[g, reach]) * scale).astype(BF16)
                dk_acc[g, reach] += dot_tn(dscores, q_s[h, mine])
                dv_acc[g, reach] += dot_tn(probs.astype(BF16), grad)
                return carry

            lax.fori_loop(0, rows // QB, attend_back, 0)

            pair_copy(h).wait_recv()

            def pair_sum(d, carry):
                total = own_part[d] + pair_recv[h, d].astype(F32)
                own_part[d] = total
                far_send[h, d] = total.astype(BF16)
                return carry

            lax.fori_loop(0, nz, pair_sum, 0)
            own_sum[h] = own_part[z]
            for step in range(1, nz):
                far_send_copy(h, lax.rem(z + step, nz)).start()
            if h == g * groups and g > 0:
                send_back(g - 1)

        for j, acc in enumerate((dk_acc, dv_acc)):
            mid_send[g, j] = acc[g, middle].astype(BF16)
            mid_copy(g, j).start()
    send_back(ng - 1)

    for h in range(heads):
        for step in range(1, nz):
            far_recv_copy(h, lax.rem(z + step, nz)).wait_recv()
        total = own_sum[h]
        for step in range(1, nz):
            total = total + far_recv[h, lax.rem(z + step, nz)].astype(F32)
        gow_ref[:, cols(h)] = total * norm

    last = pl.ds(2 * rows, rows)

    @pl.when(jnp.logical_not(has_above))
    def _():
        for g in range(ng):
            dk_ref[:, cols(g)] = (dk_acc[g, last] * scale).astype(BF16)
            dv_ref[:, cols(g)] = dv_acc[g, last].astype(BF16)

    @pl.when(has_above)
    def _():
        for g in range(ng):
            back_copy(g, 0).wait_recv()
            dk_ref[:, cols(g)] = ((dk_acc[g, last] + back_recv[g, 0].astype(F32)) * scale).astype(BF16)
            back_copy(g, 1).wait_recv()
            dv_ref[:, cols(g)] = (dv_acc[g, last] + back_recv[g, 1].astype(F32)).astype(BF16)

    @pl.when(has_above)
    def _():
        for copy in halos:
            copy.wait_send()

    @pl.when(has_below | (s == 0))
    def _():
        for copy in from_halo:
            copy.wait_send()

    for g in range(ng):
        for j in range(2):
            mid_copy(g, j).wait_send()

            @pl.when(has_below)
            def _():
                back_copy(g, j).wait_send()

    for h in range(heads):
        pair_copy(h).wait_send()
        for step in range(1, nz):
            far_send_copy(h, lax.rem(z + step, nz)).wait_send()


def shards(nz, queries, keys, values, segment, cotangent, out_weight):
    rows = queries.shape[0]
    ng = keys.shape[1] // DH
    groups = queries.shape[1] // keys.shape[1]
    heads = ng * groups
    width = cotangent.shape[1]
    part = width // (2 * nz)
    norm = (rows * 2 * nz) ** (-0.5)
    kv_block = pltpu.VMEM((ng, 2, rows, DH), BF16)
    parts = pltpu.VMEM((heads, nz, part, DH), BF16)
    dma = pltpu.SemaphoreType.DMA
    return pl.pallas_call(
        functools.partial(layer_kernel, nz, ng, groups, norm),
        out_shape=(
            jax.ShapeDtypeStruct(queries.shape, BF16),
            jax.ShapeDtypeStruct(keys.shape, BF16),
            jax.ShapeDtypeStruct(values.shape, BF16),
            jax.ShapeDtypeStruct((part, heads * DH), F32),
        ),
        in_specs=[pl.BlockSpec(memory_space=pl.ANY)] * 6,
        out_specs=[pl.BlockSpec(memory_space=pltpu.VMEM)] * 4,
        scratch_shapes=[
            pltpu.VMEM((heads, rows, DH), BF16),
            pltpu.VMEM((heads, width, DH), BF16),
            pltpu.VMEM((rows, width), BF16),
            pltpu.VMEM((width, rows), BF16),
            pltpu.VMEM((heads, rows, DH), BF16),
            pltpu.VMEM((rows, DH), BF16),
            pltpu.VMEM((ng, 3 * rows, DH), BF16),
            pltpu.VMEM((ng, 3 * rows, DH), BF16),
            pltpu.VMEM((3, 1, rows), jnp.int32),
            pltpu.VMEM((rows // QB, QB, SPAN), F32),
            pltpu.VMEM((rows // QB, QB, SPAN), F32),
            pltpu.VMEM((ng, 3 * rows, DH), F32),
            pltpu.VMEM((ng, 3 * rows, DH), F32),
            kv_block, kv_block, kv_block, kv_block,
            pltpu.VMEM((nz, part, DH), F32),
            parts, parts, parts, parts,
            pltpu.VMEM((heads, part, DH), F32),
            dma((2 + 2 * heads + 2 * ng,)),
            dma((2 * ng + 1,)), dma((2 * ng + 1,)),
            dma((2 * ng + 1,)), dma((2 * ng + 1,)),
            dma((ng, 2)), dma((ng, 2)),
            dma((ng, 2)), dma((ng, 2)),
            dma((heads,)), dma((heads,)),
            dma((heads, nz)), dma((heads, nz)),
        ],
        compiler_params=pltpu.CompilerParams(
            collective_id=0, has_side_effects=True, vmem_limit_bytes=60 * 1024 * 1024
        ),
    )(queries, keys, values, segment.reshape(1, rows), cotangent, out_weight)


def solution(mesh):
    return jax.shard_map(
        functools.partial(shards, mesh.shape["ctx"]),
        mesh=mesh,
        in_specs=(
            P(("replica", "ctx", "sub"), "head"),
            P(("replica", "ctx", "sub"), "head"),
            P(("replica", "ctx", "sub"), "head"),
            P(("replica", "ctx", "sub")),
            P(("replica", "ctx", "sub"), None),
            P(None, "head"),
        ),
        out_specs=(
            P(("replica", "ctx", "sub"), "head"),
            P(("replica", "ctx", "sub"), "head"),
            P(("replica", "ctx", "sub"), "head"),
            P(("replica", "ctx", "sub"), "head"),
        ),
        check_vma=False,
    )
```

```python
import functools

import jax
import jax.numpy as jnp
from jax import lax
from jax.experimental import pallas as pl
from jax.experimental.pallas import tpu as pltpu
from jax.sharding import PartitionSpec as P

DH = 256
WINDOW = 1024
QB = 256
SPAN = WINDOW + QB
MASKED = -1e30
MESH = pl.DeviceIdType.MESH
F32 = jnp.float32
BF16 = jnp.bfloat16


def dot_nt(a, b):
    return lax.dot_general(a, b, (((1,), (1,)), ((), ())), preferred_element_type=F32)


def dot_tn(a, b):
    return lax.dot_general(a, b, (((0,), (0,)), ((), ())), preferred_element_type=F32)


def dot_nn(a, b):
    return lax.dot_general(a, b, (((1,), (0,)), ((), ())), preferred_element_type=F32)


def layer_kernel(
    nz, ng, groups, norm,
    q_hbm, k_hbm, v_hbm, seg_hbm, cot_hbm, w_hbm,
    dq_ref, dk_ref, dv_ref, gow_ref,
    q_s, w_s, cot_s, cot_t, da_s, at_s, kall, vall, seg_s, bias_s, prob_s, dk_acc, dv_acc,
    mid_send, mid_recv, back_send, back_recv,
    own_part, pair_send, pair_recv, far_send, far_recv, relay_recv, direct_recv, own_sum,
    in_sem, halo_ss, halo_rs, fwd_ss, fwd_rs, mid_ss, mid_rs, back_ss, back_rs,
    pair_ss, pair_rs, far_ss, far_rs, relay_ss, relay_rs, direct_ss, direct_rs,
):
    heads = ng * groups
    rows = q_hbm.shape[0]
    width = cot_hbm.shape[1]
    part = width // (2 * nz)
    scale = DH ** -0.5
    z = lax.axis_index("ctx")
    s = lax.axis_index("sub")
    peer = 1 - s
    above = lax.rem(z + 1, nz)
    below = lax.rem(z + nz - 1, nz)
    has_above = z < nz - 1
    has_below = z > 0
    couple = z // 2
    odd = lax.rem(z, 2)
    partner = z + 1 - 2 * odd
    pairs = nz // 2

    def cols(h):
        return pl.ds(h * DH, DH)

    loads = []

    def load(src, dst):
        copy = pltpu.make_async_copy(src, dst, in_sem.at[len(loads)])
        copy.start()
        loads.append(copy)
        return copy

    load_seg = load(seg_hbm, seg_s.at[2])
    load_cot = load(cot_hbm, cot_s)
    load_w = [load(w_hbm.at[:, cols(h)], w_s.at[h]) for h in range(heads)]
    load_kv = [
        (
            load(k_hbm.at[:, cols(g)], kall.at[g, pl.ds(2 * rows, rows)]),
            load(v_hbm.at[:, cols(g)], vall.at[g, pl.ds(2 * rows, rows)]),
        )
        for g in range(ng)
    ]
    load_q = [load(q_hbm.at[:, cols(h)], q_s.at[h]) for h in range(heads)]

    barrier = pltpu.get_barrier_semaphore()
    for step in range(1, nz):
        pl.semaphore_signal(barrier, inc=1, device_id={"ctx": lax.rem(z + step, nz)}, device_id_type=MESH)
    pl.semaphore_signal(barrier, inc=1, device_id={"sub": peer}, device_id_type=MESH)
    pl.semaphore_wait(barrier, nz)

    def halo(i, src, dst):
        return pltpu.make_async_remote_copy(
            src_ref=src, dst_ref=dst, send_sem=halo_ss.at[i], recv_sem=halo_rs.at[i],
            device_id={"ctx": above}, device_id_type=MESH,
        )

    def forward(i, src, dst):
        return pltpu.make_async_remote_copy(
            src_ref=src, dst_ref=dst, send_sem=fwd_ss.at[i], recv_sem=fwd_rs.at[i],
            device_id={"sub": peer}, device_id_type=MESH,
        )

    first, middle = pl.ds(0, rows), pl.ds(rows, rows)
    seg_i = 2 * ng
    halos = [halo(seg_i, seg_hbm, seg_s.at[0])]
    from_own = [forward(seg_i, seg_hbm, seg_s.at[1])]
    from_halo = [forward(seg_i, seg_s.at[0], seg_s.at[1])]
    for g in range(ng):
        for j, (hbm, both) in enumerate(((k_hbm, kall), (v_hbm, vall))):
            i = 2 * g + j
            halos.append(halo(i, hbm.at[:, cols(g)], both.at[g, first]))
            from_own.append(forward(i, hbm.at[:, cols(g)], both.at[g, middle]))
            from_halo.append(forward(i, both.at[g, first], both.at[g, middle]))

    @pl.when(has_above)
    def _():
        for copy in halos:
            copy.start()

    @pl.when(s == 0)
    def _():
        for copy in from_own:
            copy.start()

    @pl.when(jnp.logical_not(has_below))
    def _():
        seg_s[0] = jnp.full((1, rows), -1, jnp.int32)
        for g in range(ng):
            kall[g, first] = jnp.zeros((rows, DH), BF16)
            vall[g, first] = jnp.zeros((rows, DH), BF16)

    @pl.when(jnp.logical_not(has_below) & (s == 0))
    def _():
        seg_s[1] = jnp.full((1, rows), -1, jnp.int32)
        for g in range(ng):
            kall[g, middle] = jnp.zeros((rows, DH), BF16)
            vall[g, middle] = jnp.zeros((rows, DH), BF16)

    def arrive(indices):
        @pl.when(has_below)
        def _():
            for i in indices:
                halos[i].wait_recv()

        @pl.when(has_below & (s == 1))
        def _():
            for i in indices:
                from_halo[i].start()

        @pl.when(has_below | (s == 1))
        def _():
            for i in indices:
                from_halo[i].wait_recv()

    load_cot.wait()
    for h in range(heads):
        load_w[h].wait()

    def attention_grad(h, carry):
        da_s[h] = dot_nn(cot_s[...], w_s[h]).astype(BF16)
        return carry

    lax.fori_loop(0, heads, attention_grad, 0)

    for j in range(width // DH):
        cot_t[pl.ds(j * DH, DH)] = cot_s[:, cols(j)].T

    load_seg.wait()
    arrive([0])
    for b in range(rows // QB):
        own = seg_s[2]
        keys_row = jnp.concatenate([seg_s[0], seg_s[1], own], axis=1)[:, b * QB : b * QB + SPAN]
        column = jnp.broadcast_to(own[:, b * QB : (b + 1) * QB].astype(F32), (128, QB)).T[:, :1]
        at_query = lax.broadcasted_iota(jnp.int32, (QB, SPAN), 0)
        at_key = lax.broadcasted_iota(jnp.int32, (QB, SPAN), 1)
        allowed = (at_key > at_query) & (at_key <= at_query + WINDOW)
        allowed = allowed & (column == keys_row.astype(F32))
        bias_s[b] = jnp.where(allowed, 0.0, MASKED)

    def mid_copy(g, j):
        return pltpu.make_async_remote_copy(
            src_ref=mid_send.at[g, j], dst_ref=mid_recv.at[g, j],
            send_sem=mid_ss.at[g, j], recv_sem=mid_rs.at[g, j],
            device_id={"sub": peer}, device_id_type=MESH,
        )

    def back_copy(g, j):
        return pltpu.make_async_remote_copy(
            src_ref=back_send.at[g, j], dst_ref=back_recv.at[g, j],
            send_sem=back_ss.at[g, j], recv_sem=back_rs.at[g, j],
            device_id={"ctx": below}, device_id_type=MESH,
        )

    def pair_copy(h):
        return pltpu.make_async_remote_copy(
            src_ref=pair_send.at[h], dst_ref=pair_recv.at[h],
            send_sem=pair_ss.at[h], recv_sem=pair_rs.at[h],
            device_id={"sub": peer}, device_id_type=MESH,
        )

    def handed(d):
        return ((odd == 0) & (d >= 2 * couple + 2)) | ((odd == 1) & (d < 2 * couple))

    def taken(d):
        return ((odd == 1) & (d >= 2 * couple + 2)) | ((odd == 0) & (d < 2 * couple))

    def relay_copy(h, d):
        return pltpu.make_async_remote_copy(
            src_ref=far_send.at[h, d], dst_ref=relay_recv.at[h, d],
            send_sem=relay_ss.at[h, d], recv_sem=relay_rs.at[h, d],
            device_id={"ctx": partner}, device_id_type=MESH,
        )

    def direct_copy(h):
        return pltpu.make_async_remote_copy(
            src_ref=far_send.at[h, partner], dst_ref=direct_recv.at[h],
            send_sem=direct_ss.at[h], recv_sem=direct_rs.at[h],
            device_id={"ctx": partner}, device_id_type=MESH,
        )

    def far_copy(h, d, slot):
        return pltpu.make_async_remote_copy(
            src_ref=far_send.at[h, d], dst_ref=far_recv.at[h, slot],
            send_sem=far_ss.at[h, d], recv_sem=far_rs.at[h, slot],
            device_id={"ctx": d}, device_id_type=MESH,
        )

    def part_rows(d, side):
        return pl.ds(pl.multiple_of((d * 2 + side) * part, 16), part)

    def send_back(g):
        for j, acc in enumerate((dk_acc, dv_acc)):
            mid_copy(g, j).wait_recv()
            other = mid_recv[g, j].astype(F32)
            back_send[g, j] = (acc[g, first] + jnp.where(s == 1, other, 0.0)).astype(BF16)

            @pl.when(has_below)
            def _():
                back_copy(g, j).start()

            last = pl.ds(2 * rows, rows)
            acc[g, last] = acc[g, last] + jnp.where(s == 0, other, 0.0)

    def attend(g, h):
        slot = h % groups

        def block(b, carry):
            mine = pl.ds(pl.multiple_of(b * QB, QB), QB)
            reach = pl.ds(pl.multiple_of(b * QB, QB), SPAN)
            scores = dot_nt(q_s[h, mine], kall[g, reach]) * scale + bias_s[b]
            top = jnp.max(scores, axis=1, keepdims=True)
            raised = jnp.exp(scores - top)
            probs = raised * (1.0 / jnp.sum(raised, axis=1, keepdims=True))
            prob_s[slot, b] = probs
            at_s[slot, mine] = dot_nn(probs.astype(BF16), vall[g, reach]).astype(BF16)
            return carry

        lax.fori_loop(0, rows // QB, block, 0)

    def attend_back(g, h):
        slot = h % groups

        def block(b, carry):
            mine = pl.ds(pl.multiple_of(b * QB, QB), QB)
            reach = pl.ds(pl.multiple_of(b * QB, QB), SPAN)
            grad = da_s[h, mine]
            probs = prob_s[slot, b]
            delta = jnp.sum(at_s[slot, mine].astype(F32) * grad.astype(F32), axis=1, keepdims=True)
            dscores = (probs * (dot_nt(grad, vall[g, reach]) - delta)).astype(BF16)
            dq_ref[mine, cols(h)] = (dot_nn(dscores, kall[g, reach]) * scale).astype(BF16)
            dk_acc[g, reach] += dot_tn(dscores, q_s[h, mine])
            dv_acc[g, reach] += dot_tn(probs.astype(BF16), grad)
            return carry

        lax.fori_loop(0, rows // QB, block, 0)

    def weight_parts(h):
        slot = h % groups

        def peers(d, carry):
            pair_send[h, d] = dot_nn(cot_t[part_rows(d, peer)], at_s[slot]).astype(BF16)
            return carry

        lax.fori_loop(0, nz, peers, 0)
        pair_copy(h).start()

        def owns(d, carry):
            own_part[h % 2, d] = dot_nn(cot_t[part_rows(d, s)], at_s[slot])
            return carry

        lax.fori_loop(0, nz, owns, 0)

    def weight_out(h):
        pair_copy(h).wait_recv()

        def both(d, carry):
            far_send[h, d] = (own_part[h % 2, d] + pair_recv[h, d].astype(F32)).astype(BF16)
            return carry

        lax.fori_loop(0, nz, both, 0)
        for d in range(nz):

            @pl.when(handed(d))
            def _():
                relay_copy(h, d).start()

        direct_copy(h).start()
        own_sum[h] = own_part[h % 2, z] + pair_recv[h, z].astype(F32)

    def weight_relay(h):
        for d in range(nz):

            @pl.when(taken(d))
            def _():
                relay_copy(h, d).wait_recv()
                far_send[h, d] = (far_send[h, d].astype(F32) + relay_recv[h, d].astype(F32)).astype(BF16)
                far_copy(h, d, couple).start()

    for g in range(ng):
        load_kv[g][0].wait()
        load_kv[g][1].wait()
        arrive([1 + 2 * g, 2 + 2 * g])
        dk_acc[g] = jnp.zeros((3 * rows, DH), F32)
        dv_acc[g] = jnp.zeros((3 * rows, DH), F32)
        here = range(g * groups, (g + 1) * groups)
        for h in here:
            load_q[h].wait()
            attend(g, h)
            if h > here[0]:
                weight_out(h - 1)
            weight_parts(h)
            if g > 0:
                if h == here[0]:
                    send_back(g - 1)
                weight_relay(h - groups)
        for h in here:
            attend_back(g, h)
            if h == here[0]:
                weight_out(here[-1])
        for j, acc in enumerate((dk_acc, dv_acc)):
            mid_send[g, j] = acc[g, middle].astype(BF16)
            mid_copy(g, j).start()
    send_back(ng - 1)
    for h in range(heads - groups, heads):
        weight_relay(h)

    for h in range(heads):
        direct_copy(h).wait_recv()
        own_sum[h] = own_sum[h] + direct_recv[h].astype(F32)
        for slot in range(pairs):

            @pl.when(couple != slot)
            def _():
                far_copy(h, 0, slot).wait_recv()
                own_sum[h] = own_sum[h] + far_recv[h, slot].astype(F32)

        gow_ref[:, cols(h)] = own_sum[h] * norm

    last = pl.ds(2 * rows, rows)

    @pl.when(jnp.logical_not(has_above))
    def _():
        for g in range(ng):
            dk_ref[:, cols(g)] = (dk_acc[g, last] * scale).astype(BF16)
            dv_ref[:, cols(g)] = dv_acc[g, last].astype(BF16)

    @pl.when(has_above)
    def _():
        for g in range(ng):
            back_copy(g, 0).wait_recv()
            dk_ref[:, cols(g)] = ((dk_acc[g, last] + back_recv[g, 0].astype(F32)) * scale).astype(BF16)
            back_copy(g, 1).wait_recv()
            dv_ref[:, cols(g)] = (dv_acc[g, last] + back_recv[g, 1].astype(F32)).astype(BF16)

    @pl.when(has_above)
    def _():
        for copy in halos:
            copy.wait_send()

    @pl.when(has_below | (s == 0))
    def _():
        for copy in from_halo:
            copy.wait_send()

    for g in range(ng):
        for j in range(2):
            mid_copy(g, j).wait_send()

            @pl.when(has_below)
            def _():
                back_copy(g, j).wait_send()

    for h in range(heads):
        pair_copy(h).wait_send()
        direct_copy(h).wait_send()
        for d in range(nz):

            @pl.when(handed(d))
            def _():
                relay_copy(h, d).wait_send()

            @pl.when(taken(d))
            def _():
                far_copy(h, d, couple).wait_send()


def shards(nz, queries, keys, values, segment, cotangent, out_weight):
    rows = queries.shape[0]
    ng = keys.shape[1] // DH
    groups = queries.shape[1] // keys.shape[1]
    heads = ng * groups
    width = cotangent.shape[1]
    part = width // (2 * nz)
    norm = (rows * 2 * nz) ** (-0.5)
    kv_block = pltpu.VMEM((ng, 2, rows, DH), BF16)
    parts = pltpu.VMEM((heads, nz, part, DH), BF16)
    dma = pltpu.SemaphoreType.DMA
    return pl.pallas_call(
        functools.partial(layer_kernel, nz, ng, groups, norm),
        out_shape=(
            jax.ShapeDtypeStruct(queries.shape, BF16),
            jax.ShapeDtypeStruct(keys.shape, BF16),
            jax.ShapeDtypeStruct(values.shape, BF16),
            jax.ShapeDtypeStruct((part, heads * DH), F32),
        ),
        in_specs=[pl.BlockSpec(memory_space=pl.ANY)] * 6,
        out_specs=[pl.BlockSpec(memory_space=pltpu.VMEM)] * 4,
        scratch_shapes=[
            pltpu.VMEM((heads, rows, DH), BF16),
            pltpu.VMEM((heads, width, DH), BF16),
            pltpu.VMEM((rows, width), BF16),
            pltpu.VMEM((width, rows), BF16),
            pltpu.VMEM((heads, rows, DH), BF16),
            pltpu.VMEM((groups, rows, DH), BF16),
            pltpu.VMEM((ng, 3 * rows, DH), BF16),
            pltpu.VMEM((ng, 3 * rows, DH), BF16),
            pltpu.VMEM((3, 1, rows), jnp.int32),
            pltpu.VMEM((rows // QB, QB, SPAN), F32),
            pltpu.VMEM((groups, rows // QB, QB, SPAN), F32),
            pltpu.VMEM((ng, 3 * rows, DH), F32),
            pltpu.VMEM((ng, 3 * rows, DH), F32),
            kv_block, kv_block, kv_block, kv_block,
            pltpu.VMEM((2, nz, part, DH), F32),
            parts, parts, parts,
            pltpu.VMEM((heads, nz // 2, part, DH), BF16),
            parts,
            pltpu.VMEM((heads, part, DH), BF16),
            pltpu.VMEM((heads, part, DH), F32),
            dma((2 + 2 * heads + 2 * ng,)),
            dma((2 * ng + 1,)), dma((2 * ng + 1,)),
            dma((2 * ng + 1,)), dma((2 * ng + 1,)),
            dma((ng, 2)), dma((ng, 2)),
            dma((ng, 2)), dma((ng, 2)),
            dma((heads,)), dma((heads,)),
            dma((heads, nz)), dma((heads, nz // 2)),
            dma((heads, nz)), dma((heads, nz)),
            dma((heads,)), dma((heads,)),
        ],
        compiler_params=pltpu.CompilerParams(
            collective_id=0, has_side_effects=True, vmem_limit_bytes=60 * 1024 * 1024
        ),
    )(queries, keys, values, segment.reshape(1, rows), cotangent, out_weight)


def solution(mesh):
    return jax.shard_map(
        functools.partial(shards, mesh.shape["ctx"]),
        mesh=mesh,
        in_specs=(
            P(("replica", "ctx", "sub"), "head"),
            P(("replica", "ctx", "sub"), "head"),
            P(("replica", "ctx", "sub"), "head"),
            P(("replica", "ctx", "sub")),
            P(("replica", "ctx", "sub"), None),
            P(None, "head"),
        ),
        out_specs=(
            P(("replica", "ctx", "sub"), "head"),
            P(("replica", "ctx", "sub"), "head"),
            P(("replica", "ctx", "sub"), "head"),
            P(("replica", "ctx", "sub"), "head"),
        ),
        check_vma=False,
    )
```

```python
import functools

import jax
import jax.numpy as jnp
from jax import lax
from jax.experimental import pallas as pl
from jax.experimental.pallas import tpu as pltpu
from jax.sharding import PartitionSpec as P

DH = 256
WINDOW = 1024
QB = 256
SPAN = WINDOW + QB
MASKED = -1e30
MESH = pl.DeviceIdType.MESH
F32 = jnp.float32
BF16 = jnp.bfloat16


def dot_nt(a, b):
    return lax.dot_general(a, b, (((1,), (1,)), ((), ())), preferred_element_type=F32)


def dot_tn(a, b):
    return lax.dot_general(a, b, (((0,), (0,)), ((), ())), preferred_element_type=F32)


def dot_nn(a, b):
    return lax.dot_general(a, b, (((1,), (0,)), ((), ())), preferred_element_type=F32)


def layer_kernel(
    nz, ng, groups, norm,
    q_hbm, k_hbm, v_hbm, seg_hbm, cot_hbm, w_hbm,
    dq_ref, dk_ref, dv_ref, gow_ref,
    q_s, w_s, cot_s, cot_t, da_s, at_s, kall, vall, seg_s, bias_s, prob_s, dk_acc, dv_acc,
    mid_send, mid_recv, back_send, back_recv,
    own_part, pair_send, pair_recv, far_send, far_recv, relay_recv, direct_recv, own_sum,
    in_sem, halo_ss, halo_rs, fwd_ss, fwd_rs, mid_ss, mid_rs, back_ss, back_rs,
    pair_ss, pair_rs, far_ss, far_rs, relay_ss, relay_rs, direct_ss, direct_rs,
):
    heads = ng * groups
    rows = q_hbm.shape[0]
    width = cot_hbm.shape[1]
    part = width // (2 * nz)
    scale = DH ** -0.5
    z = lax.axis_index("ctx")
    s = lax.axis_index("sub")
    peer = 1 - s
    above = lax.rem(z + 1, nz)
    below = lax.rem(z + nz - 1, nz)
    has_above = z < nz - 1
    has_below = z > 0
    couple = z // 2
    odd = lax.rem(z, 2)
    partner = z + 1 - 2 * odd
    pairs = nz // 2

    def cols(h):
        return pl.ds(h * DH, DH)

    loads = []

    def load(src, dst):
        copy = pltpu.make_async_copy(src, dst, in_sem.at[len(loads)])
        copy.start()
        loads.append(copy)
        return copy

    load_seg = load(seg_hbm, seg_s.at[2])
    load_cot = load(cot_hbm, cot_s)
    load_w = [load(w_hbm.at[:, cols(h)], w_s.at[h]) for h in range(heads)]
    load_kv = [
        (
            load(k_hbm.at[:, cols(g)], kall.at[g, pl.ds(2 * rows, rows)]),
            load(v_hbm.at[:, cols(g)], vall.at[g, pl.ds(2 * rows, rows)]),
        )
        for g in range(ng)
    ]
    load_q = [load(q_hbm.at[:, cols(h)], q_s.at[h]) for h in range(heads)]

    barrier = pltpu.get_barrier_semaphore()
    for step in range(1, nz):
        pl.semaphore_signal(barrier, inc=1, device_id={"ctx": lax.rem(z + step, nz)}, device_id_type=MESH)
    pl.semaphore_signal(barrier, inc=1, device_id={"sub": peer}, device_id_type=MESH)
    pl.semaphore_wait(barrier, nz)

    def halo(i, src, dst):
        return pltpu.make_async_remote_copy(
            src_ref=src, dst_ref=dst, send_sem=halo_ss.at[i], recv_sem=halo_rs.at[i],
            device_id={"ctx": above}, device_id_type=MESH,
        )

    def forward(i, src, dst):
        return pltpu.make_async_remote_copy(
            src_ref=src, dst_ref=dst, send_sem=fwd_ss.at[i], recv_sem=fwd_rs.at[i],
            device_id={"sub": peer}, device_id_type=MESH,
        )

    first, middle = pl.ds(0, rows), pl.ds(rows, rows)
    seg_i = 2 * ng
    halos = [halo(seg_i, seg_hbm, seg_s.at[0])]
    from_own = [forward(seg_i, seg_hbm, seg_s.at[1])]
    from_halo = [forward(seg_i, seg_s.at[0], seg_s.at[1])]
    for g in range(ng):
        for j, (hbm, both) in enumerate(((k_hbm, kall), (v_hbm, vall))):
            i = 2 * g + j
            halos.append(halo(i, hbm.at[:, cols(g)], both.at[g, first]))
            from_own.append(forward(i, hbm.at[:, cols(g)], both.at[g, middle]))
            from_halo.append(forward(i, both.at[g, first], both.at[g, middle]))

    @pl.when(has_above)
    def _():
        for copy in halos[:3]:
            copy.start()

    @pl.when(s == 0)
    def _():
        for copy in from_own:
            copy.start()

    @pl.when(jnp.logical_not(has_below))
    def _():
        seg_s[0] = jnp.full((1, rows), -1, jnp.int32)
        for g in range(ng):
            kall[g, first] = jnp.zeros((rows, DH), BF16)
            vall[g, first] = jnp.zeros((rows, DH), BF16)

    @pl.when(jnp.logical_not(has_below) & (s == 0))
    def _():
        seg_s[1] = jnp.full((1, rows), -1, jnp.int32)
        for g in range(ng):
            kall[g, middle] = jnp.zeros((rows, DH), BF16)
            vall[g, middle] = jnp.zeros((rows, DH), BF16)

    def arrive(indices):
        @pl.when(has_below)
        def _():
            for i in indices:
                halos[i].wait_recv()

        @pl.when(has_below & (s == 1))
        def _():
            for i in indices:
                from_halo[i].start()

        @pl.when(has_below | (s == 1))
        def _():
            for i in indices:
                from_halo[i].wait_recv()

    load_cot.wait()
    for h in range(heads):
        load_w[h].wait()

    def attention_grad(h, carry):
        da_s[h] = dot_nn(cot_s[...], w_s[h]).astype(BF16)
        return carry

    lax.fori_loop(0, heads, attention_grad, 0)

    for j in range(width // DH):
        cot_t[pl.ds(j * DH, DH)] = cot_s[:, cols(j)].T

    for g in range(1, ng):

        @pl.when(has_above)
        def _():
            halos[2 * g - 1].wait_send()
            halos[2 * g].wait_send()
            halos[2 * g + 1].start()
            halos[2 * g + 2].start()

    load_seg.wait()
    arrive([0])
    for b in range(rows // QB):
        own = seg_s[2]
        keys_row = jnp.concatenate([seg_s[0], seg_s[1], own], axis=1)[:, b * QB : b * QB + SPAN]
        column = jnp.broadcast_to(own[:, b * QB : (b + 1) * QB].astype(F32), (128, QB)).T[:, :1]
        at_query = lax.broadcasted_iota(jnp.int32, (QB, SPAN), 0)
        at_key = lax.broadcasted_iota(jnp.int32, (QB, SPAN), 1)
        allowed = (at_key > at_query) & (at_key <= at_query + WINDOW)
        allowed = allowed & (column == keys_row.astype(F32))
        bias_s[b] = jnp.where(allowed, 0.0, MASKED)

    def mid_copy(g, j):
        return pltpu.make_async_remote_copy(
            src_ref=mid_send.at[g, j], dst_ref=mid_recv.at[g, j],
            send_sem=mid_ss.at[g, j], recv_sem=mid_rs.at[g, j],
            device_id={"sub": peer}, device_id_type=MESH,
        )

    def back_copy(g, j):
        return pltpu.make_async_remote_copy(
            src_ref=back_send.at[g, j], dst_ref=back_recv.at[g, j],
            send_sem=back_ss.at[g, j], recv_sem=back_rs.at[g, j],
            device_id={"ctx": below}, device_id_type=MESH,
        )

    def pair_copy(h):
        return pltpu.make_async_remote_copy(
            src_ref=pair_send.at[h], dst_ref=pair_recv.at[h],
            send_sem=pair_ss.at[h], recv_sem=pair_rs.at[h],
            device_id={"sub": peer}, device_id_type=MESH,
        )

    def handed(d):
        return ((odd == 0) & (d >= 2 * couple + 2)) | ((odd == 1) & (d < 2 * couple))

    def taken(d):
        return ((odd == 1) & (d >= 2 * couple + 2)) | ((odd == 0) & (d < 2 * couple))

    def relay_copy(h, d):
        return pltpu.make_async_remote_copy(
            src_ref=far_send.at[h, d], dst_ref=relay_recv.at[h, d],
            send_sem=relay_ss.at[h, d], recv_sem=relay_rs.at[h, d],
            device_id={"ctx": partner}, device_id_type=MESH,
        )

    def direct_copy(h):
        return pltpu.make_async_remote_copy(
            src_ref=far_send.at[h, partner], dst_ref=direct_recv.at[h],
            send_sem=direct_ss.at[h], recv_sem=direct_rs.at[h],
            device_id={"ctx": partner}, device_id_type=MESH,
        )

    def far_copy(h, d, slot):
        return pltpu.make_async_remote_copy(
            src_ref=far_send.at[h, d], dst_ref=far_recv.at[h, slot],
            send_sem=far_ss.at[h, d], recv_sem=far_rs.at[h, slot],
            device_id={"ctx": d}, device_id_type=MESH,
        )

    def part_rows(d, side):
        return pl.ds(pl.multiple_of((d * 2 + side) * part, 16), part)

    def send_back(g):
        for j, acc in enumerate((dk_acc, dv_acc)):
            mid_copy(g, j).wait_recv()
            other = mid_recv[g, j].astype(F32)
            back_send[g, j] = (acc[g, first] + jnp.where(s == 1, other, 0.0)).astype(BF16)

            @pl.when(has_below)
            def _():
                back_copy(g, j).start()

            last = pl.ds(2 * rows, rows)
            acc[g, last] = acc[g, last] + jnp.where(s == 0, other, 0.0)

    def attend(g, h):
        slot = h % groups

        def block(b, carry):
            mine = pl.ds(pl.multiple_of(b * QB, QB), QB)
            reach = pl.ds(pl.multiple_of(b * QB, QB), SPAN)
            scores = dot_nt(q_s[h, mine], kall[g, reach]) * scale + bias_s[b]
            top = jnp.max(scores, axis=1, keepdims=True)
            raised = jnp.exp(scores - top)
            probs = raised * (1.0 / jnp.sum(raised, axis=1, keepdims=True))
            prob_s[slot, b] = probs
            at_s[slot, mine] = dot_nn(probs.astype(BF16), vall[g, reach]).astype(BF16)
            return carry

        lax.fori_loop(0, rows // QB, block, 0)

    def attend_back(g, h):
        slot = h % groups

        def block(b, carry):
            mine = pl.ds(pl.multiple_of(b * QB, QB), QB)
            reach = pl.ds(pl.multiple_of(b * QB, QB), SPAN)
            grad = da_s[h, mine]
            probs = prob_s[slot, b]
            delta = jnp.sum(at_s[slot, mine].astype(F32) * grad.astype(F32), axis=1, keepdims=True)
            dscores = (probs * (dot_nt(grad, vall[g, reach]) - delta)).astype(BF16)
            dq_ref[mine, cols(h)] = (dot_nn(dscores, kall[g, reach]) * scale).astype(BF16)
            dk_acc[g, reach] += dot_tn(dscores, q_s[h, mine])
            dv_acc[g, reach] += dot_tn(probs.astype(BF16), grad)
            return carry

        lax.fori_loop(0, rows // QB, block, 0)

    def weight_parts(h):
        slot = h % groups

        def peers(d, carry):
            pair_send[h, d] = dot_nn(cot_t[part_rows(d, peer)], at_s[slot]).astype(BF16)
            return carry

        lax.fori_loop(0, nz, peers, 0)
        pair_copy(h).start()

        def owns(d, carry):
            own_part[h % 2, d] = dot_nn(cot_t[part_rows(d, s)], at_s[slot])
            return carry

        lax.fori_loop(0, nz, owns, 0)

    def weight_out(h):
        pair_copy(h).wait_recv()

        def both(d, carry):
            far_send[h, d] = (own_part[h % 2, d] + pair_recv[h, d].astype(F32)).astype(BF16)
            return carry

        lax.fori_loop(0, nz, both, 0)
        for d in range(nz):

            @pl.when(handed(d))
            def _():
                relay_copy(h, d).start()

        if h > 0:
            direct_copy(h - 1).start()
        if h == heads - 1:
            direct_copy(h).start()
        own_sum[h] = own_part[h % 2, z] + pair_recv[h, z].astype(F32)

    def weight_relay(h):
        for d in range(nz):

            @pl.when(taken(d))
            def _():
                relay_copy(h, d).wait_recv()
                far_send[h, d] = (far_send[h, d].astype(F32) + relay_recv[h, d].astype(F32)).astype(BF16)
                far_copy(h, d, couple).start()

    for g in range(ng):
        load_kv[g][0].wait()
        load_kv[g][1].wait()
        arrive([1 + 2 * g, 2 + 2 * g])
        dk_acc[g] = jnp.zeros((3 * rows, DH), F32)
        dv_acc[g] = jnp.zeros((3 * rows, DH), F32)
        here = range(g * groups, (g + 1) * groups)
        for h in here:
            load_q[h].wait()
            attend(g, h)
            if h > here[0]:
                weight_out(h - 1)
            weight_parts(h)
            if g > 0:
                if h == here[0]:
                    send_back(g - 1)
                weight_relay(h - groups)
        for h in here:
            attend_back(g, h)
            if h == here[0]:
                weight_out(here[-1])
        for j, acc in enumerate((dk_acc, dv_acc)):
            mid_send[g, j] = acc[g, middle].astype(BF16)
            mid_copy(g, j).start()
    send_back(ng - 1)
    for h in range(heads - groups, heads):
        weight_relay(h)

    for h in range(heads):
        direct_copy(h).wait_recv()
        own_sum[h] = own_sum[h] + direct_recv[h].astype(F32)
        for slot in range(pairs):

            @pl.when(couple != slot)
            def _():
                far_copy(h, 0, slot).wait_recv()
                own_sum[h] = own_sum[h] + far_recv[h, slot].astype(F32)

        gow_ref[:, cols(h)] = own_sum[h] * norm

    last = pl.ds(2 * rows, rows)

    @pl.when(jnp.logical_not(has_above))
    def _():
        for g in range(ng):
            dk_ref[:, cols(g)] = (dk_acc[g, last] * scale).astype(BF16)
            dv_ref[:, cols(g)] = dv_acc[g, last].astype(BF16)

    @pl.when(has_above)
    def _():
        for g in range(ng):
            back_copy(g, 0).wait_recv()
            dk_ref[:, cols(g)] = ((dk_acc[g, last] + back_recv[g, 0].astype(F32)) * scale).astype(BF16)
            back_copy(g, 1).wait_recv()
            dv_ref[:, cols(g)] = (dv_acc[g, last] + back_recv[g, 1].astype(F32)).astype(BF16)

    @pl.when(has_above)
    def _():
        for copy in [halos[0]] + halos[2 * ng - 1 :]:
            copy.wait_send()

    @pl.when(has_below | (s == 0))
    def _():
        for copy in from_halo:
            copy.wait_send()

    for g in range(ng):
        for j in range(2):
            mid_copy(g, j).wait_send()

            @pl.when(has_below)
            def _():
                back_copy(g, j).wait_send()

    for h in range(heads):
        pair_copy(h).wait_send()
        direct_copy(h).wait_send()
        for d in range(nz):

            @pl.when(handed(d))
            def _():
                relay_copy(h, d).wait_send()

            @pl.when(taken(d))
            def _():
                far_copy(h, d, couple).wait_send()


def store_kernel(*refs):
    for src, dst in zip(refs[:4], refs[4:]):
        dst[...] = src[...]


def shards(nz, queries, keys, values, segment, cotangent, out_weight):
    rows = queries.shape[0]
    ng = keys.shape[1] // DH
    groups = queries.shape[1] // keys.shape[1]
    heads = ng * groups
    width = cotangent.shape[1]
    part = width // (2 * nz)
    norm = (rows * 2 * nz) ** (-0.5)
    kv_block = pltpu.VMEM((ng, 2, rows, DH), BF16)
    parts = pltpu.VMEM((heads, nz, part, DH), BF16)
    dma = pltpu.SemaphoreType.DMA
    shapes = (
        jax.ShapeDtypeStruct(queries.shape, BF16),
        jax.ShapeDtypeStruct(keys.shape, BF16),
        jax.ShapeDtypeStruct(values.shape, BF16),
        jax.ShapeDtypeStruct((part, heads * DH), F32),
    )
    grads = pl.pallas_call(
        functools.partial(layer_kernel, nz, ng, groups, norm),
        out_shape=shapes,
        in_specs=[pl.BlockSpec(memory_space=pl.ANY)] * 6,
        out_specs=[pl.BlockSpec(memory_space=pltpu.VMEM)] * 4,
        scratch_shapes=[
            pltpu.VMEM((heads, rows, DH), BF16),
            pltpu.VMEM((heads, width, DH), BF16),
            pltpu.VMEM((rows, width), BF16),
            pltpu.VMEM((width, rows), BF16),
            pltpu.VMEM((heads, rows, DH), BF16),
            pltpu.VMEM((groups, rows, DH), BF16),
            pltpu.VMEM((ng, 3 * rows, DH), BF16),
            pltpu.VMEM((ng, 3 * rows, DH), BF16),
            pltpu.VMEM((3, 1, rows), jnp.int32),
            pltpu.VMEM((rows // QB, QB, SPAN), F32),
            pltpu.VMEM((groups, rows // QB, QB, SPAN), F32),
            pltpu.VMEM((ng, 3 * rows, DH), F32),
            pltpu.VMEM((ng, 3 * rows, DH), F32),
            kv_block, kv_block, kv_block, kv_block,
            pltpu.VMEM((2, nz, part, DH), F32),
            parts, parts, parts,
            pltpu.VMEM((heads, nz // 2, part, DH), BF16),
            parts,
            pltpu.VMEM((heads, part, DH), BF16),
            pltpu.VMEM((heads, part, DH), F32),
            dma((2 + 2 * heads + 2 * ng,)),
            dma((2 * ng + 1,)), dma((2 * ng + 1,)),
            dma((2 * ng + 1,)), dma((2 * ng + 1,)),
            dma((ng, 2)), dma((ng, 2)),
            dma((ng, 2)), dma((ng, 2)),
            dma((heads,)), dma((heads,)),
            dma((heads, nz)), dma((heads, nz // 2)),
            dma((heads, nz)), dma((heads, nz)),
            dma((heads,)), dma((heads,)),
        ],
        compiler_params=pltpu.CompilerParams(
            collective_id=0, has_side_effects=True, vmem_limit_bytes=60 * 1024 * 1024
        ),
    )(queries, keys, values, segment.reshape(1, rows), cotangent, out_weight)
    halves = [pl.BlockSpec((a.shape[0] // 2, a.shape[1]), lambda i: (i, 0)) for a in shapes]
    return pl.pallas_call(
        store_kernel, grid=(2,), out_shape=shapes, in_specs=halves, out_specs=halves,
    )(*grads)


def solution(mesh):
    return jax.shard_map(
        functools.partial(shards, mesh.shape["ctx"]),
        mesh=mesh,
        in_specs=(
            P(("replica", "ctx", "sub"), "head"),
            P(("replica", "ctx", "sub"), "head"),
            P(("replica", "ctx", "sub"), "head"),
            P(("replica", "ctx", "sub")),
            P(("replica", "ctx", "sub"), None),
            P(None, "head"),
        ),
        out_specs=(
            P(("replica", "ctx", "sub"), "head"),
            P(("replica", "ctx", "sub"), "head"),
            P(("replica", "ctx", "sub"), "head"),
            P(("replica", "ctx", "sub"), "head"),
        ),
        check_vma=False,
    )
```
